32 devices in a mesh: cube: 16 (over z, y, x), front: 2 (over core).
Axes of the slice: x: 2, y: 2, z: 4, core: 2. Of those that a mesh axis runs over, the one named last changes fastest.
Arguments:
- elem_loads: float32 [64, 8192], P(None, ('cube', 'front')), may hold values from -6 to 6
- elem_owner: int32 [8192, 1], P(('cube', 'front')), may hold values from 0 to 31; in each aligned block of 256 rows (0 to 255, 256 to 511, ...) at most 16 rows name the same one
- elem_row: int32 [8192], P(('cube', 'front')), may hold values from 0 to 1023
- sep_loads: float32 [4, 64, 512], P(None, None, ('cube', 'front')), may hold values from -6 to 6
- leaf_inverse: float32 [32768, 1024], P(('cube', 'front'))
- leaf_coupling: float32 [64, 32768], P(None, ('cube', 'front')), may hold values from -0.09375 to 0.09375
- coupling0: float32 [512, 512], P(None, ('cube', 'front')), may hold values from -0.25 to 0.25
- coupling1: float32 [256, 512], P(None, ('cube', 'front')), may hold values from -0.375 to 0.375
- coupling2: float32 [128, 512], P(None, ('cube', 'front')), may hold values from -0.5 to 0.5
- inverse0: float32 [512, 512], P(('cube', 'front'))
- inverse1: float32 [512, 256], P(('cube', 'front'))
- inverse2: float32 [512, 128], P(('cube', 'front'))
- inverse3: float32 [512, 64], P(('cube', 'front'))
Outputs:
- leaf_solution: float32 [64, 32768], P(None, ('cube', 'front'))
- sep_solution: float32 [4, 64, 512], P(None, None, ('cube', 'front'))
The draws below stay inside these ranges and needn't reach their ends.
Inputs may be any that keep to these rules, and one draw needn't show every extreme that they name: `elem_owner`: among the element rows of one device, at most 16 name the same owner, a bound that some block reaches.
All inputs are finite; a program needn't handle non-finite values.
Results may differ from the reference program's by a relative error of at most 0.00012.
Values sent between devices are 32-bit elements; how exact they have to be, the bound alone decides.
A program may use at most 64 MiB of HBM per device.

```python
import math
import jax
import jax.numpy as jnp
import numpy as np
from jax import lax

NRHS = 64
LEAF = 1024
SR = 16
E_DEV = 256
LEVELS = 4
SEP0 = 512
SEP1 = 256
SEP2 = 128
SEP3 = 64
ELEMS = 8192
CAP = 16
DEVICES = 32


def lower_block(key, rows, block):
    first, second = jax.random.split(key)
    local = jnp.arange(rows)[:, None] % block
    column = jnp.arange(block)[None, :]
    diagonal = jax.random.uniform(first, (rows, block), jnp.float32, 0.5, 1.5)
    below = jax.random.normal(second, (rows, block), jnp.float32) * (0.6 / math.sqrt(block))
    return jnp.where(column == local, diagonal, jnp.where(column < local, below, 0.0))


def draw_leaf_inverse(key, part):
    return lower_block(key, LEAF * DEVICES, LEAF)


def draw_inverse0(key, part):
    return lower_block(key, SEP0, SEP0)


def draw_inverse1(key, part):
    return lower_block(key, SEP0, SEP1)


def draw_inverse2(key, part):
    return lower_block(key, SEP0, SEP2)


def draw_inverse3(key, part):
    return lower_block(key, SEP0, SEP3)


def with_ends(entries, rng, least, high):
    longest = entries.shape.index(max(entries.shape))
    spots = []
    for shift in (0, 1):
        where = [jax.random.randint(jax.random.fold_in(rng, axis), (), 0, length) for axis, length in enumerate(entries.shape)]
        where[longest] = (where[longest] + shift) % entries.shape[longest]
        spots.append(tuple(where))
    return entries.at[spots[0]].set(least).at[spots[1]].set(high)


def shard_levels(own_key, shape, cuts, least, largest):
    level, own = 1.0, jax.random.fold_in(own_key, 6)
    for dim, blocks in cuts:
        steps = jnp.exp(jax.random.uniform(jax.random.fold_in(own, dim), (blocks,), jnp.float32, least / len(cuts), largest / len(cuts)))
        level = level * jnp.repeat(steps, shape[dim] // blocks).reshape([-1 if axis == dim else 1 for axis in range(len(shape))])
    return level


def shared_out(stream_key, own, number, rows, amount, top, most, slope):
    ranking = jax.random.permutation(stream_key, amount)
    crowded, common = load_shares(amount, rows * top, most, slope, True), load_shares(amount, rows * top, most, slope, False)
    places = jnp.arange(amount)

    def named(lengths, rotation):
        used = int((lengths > 0).sum())
        fixed = max(1, used // 4)
        passed = fixed + (places - fixed + rotation * (used - fixed)) % max(1, amount - fixed)
        return jnp.zeros((amount,), jnp.int32).at[ranking[jnp.where(places < fixed, places, passed)]].set(jnp.asarray(lengths, jnp.int32))

    lengths = jnp.where(number % 4 == 0, named(crowded, number // 4), named(common, number - number // 4 - 1))
    mixed = jax.random.permutation(jax.random.fold_in(own, 3), amount)
    donor, taker = mixed[0:amount // 2 * 2:2], mixed[1:amount // 2 * 2:2]
    room = jnp.minimum(lengths[donor] - 1, most - lengths[taker]) // 2
    room = jnp.where((donor == ranking[0]) | (taker == ranking[0]) | (lengths[taker] == 0), 0, jnp.maximum(room, 0))
    passed = jax.random.randint(jax.random.fold_in(own, 4), (amount // 2,), 0, 1 << 20) % (room + 1)
    lengths = lengths.at[donor].add(-passed).at[taker].add(passed)
    items = jnp.searchsorted(jnp.cumsum(lengths), jnp.arange(rows * top), side="right").astype(jnp.int32)
    table = items.reshape(top, rows).T
    table = table[jax.random.permutation(jax.random.fold_in(own, 1), rows)]
    rotation = jax.random.randint(jax.random.fold_in(own, 2), (rows, 1), 0, top)
    return jnp.take_along_axis(table, (jnp.arange(top)[None, :] + rotation) % top, axis=1)


def load_shares(count, total, most, skew, full):
    weights = [(1 << 20) // math.isqrt(grade ** skew) + 1 for grade in range(1, count + 1)]
    largest = most if full else min(most, max(-(-total // count), total * weights[0] // sum(weights)))
    least = 1 if total - largest >= count - 1 else 0
    holding, rest = [largest] + [least] * (count - 1), total - largest - least * (count - 1)
    while rest > 0:
        candidates = [i for i in range(1, count) if holding[i] < largest] or [i for i in range(1, count) if holding[i] < most]
        mass, remaining = sum([weights[i] for i in candidates]), rest
        for i in candidates:
            more = min(most - holding[i], max(1, remaining * weights[i] // mass), rest)
            holding[i] = holding[i] + more
            rest = rest - more
    return np.array(holding)


def bell_draw(stream_key, shape, scale, most, cuts=(), held_as=jnp.bfloat16):
    array = jax.random.normal(stream_key, shape, jnp.float32) * scale
    if len(cuts) > 0:
        array = shard_levels(stream_key, shape, cuts, -0.22, 0.18) * array
    return jnp.clip(array, min=-most, max=most).astype(held_as)


def setup_inputs(seed: int = 0) -> dict:
    keys = jax.random.split(jax.random.key(seed), 14)
    elem_loads = bell_draw(keys[0], (NRHS, ELEMS), 1.0, 6.0, ((1, 32),), jnp.float32)
    elem_owner_keys = jax.random.split(jax.random.fold_in(keys[1], 1), ELEMS // E_DEV)
    elem_owner_turns = jax.random.permutation(jax.random.fold_in(keys[1], 3), ELEMS // E_DEV)
    elem_owner = jax.vmap(lambda own, number: shared_out(jax.random.fold_in(keys[1], 2), own, number, E_DEV, DEVICES, 1, CAP, 2))(elem_owner_keys, elem_owner_turns).reshape((ELEMS, 1))
    elem_row = with_ends(jax.random.randint(keys[2], (ELEMS,), 0, LEAF), jax.random.fold_in(keys[2], 1), 0, LEAF - 1).astype(jnp.int32)
    sep_loads = bell_draw(keys[3], (LEVELS, NRHS, SEP0), 1.0, 6.0, ((2, 32),), jnp.float32)
    leaf_inverse = draw_leaf_inverse(jax.random.fold_in(keys[13], 71), 0)
    leaf_coupling = bell_draw(keys[5], (SEP3, LEAF * DEVICES), (LEAF * DEVICES // 8) ** -0.5, 0.09375, ((1, 32),), jnp.float32)
    coupling0 = bell_draw(keys[6], (SEP0, SEP0), SEP0 ** -0.5, 0.25, ((1, 32),), jnp.float32)
    coupling1 = bell_draw(keys[7], (SEP1, SEP0), SEP1 ** -0.5, 0.375, ((1, 32),), jnp.float32)
    coupling2 = bell_draw(keys[8], (SEP2, SEP0), SEP2 ** -0.5, 0.5, ((1, 32),), jnp.float32)
    inverse0 = draw_inverse0(jax.random.fold_in(keys[13], 71), 0)
    inverse1 = draw_inverse1(jax.random.fold_in(keys[13], 71), 0)
    inverse2 = draw_inverse2(jax.random.fold_in(keys[13], 71), 0)
    inverse3 = draw_inverse3(jax.random.fold_in(keys[13], 71), 0)
    return dict(elem_loads=elem_loads, elem_owner=elem_owner, elem_row=elem_row, sep_loads=sep_loads, leaf_inverse=leaf_inverse, leaf_coupling=leaf_coupling, coupling0=coupling0, coupling1=coupling1, coupling2=coupling2, inverse0=inverse0, inverse1=inverse1, inverse2=inverse2, inverse3=inverse3)


HIGH = lax.Precision.HIGHEST


def reference(elem_loads, elem_owner, elem_row, sep_loads, leaf_inverse, leaf_coupling, coupling0, coupling1, coupling2, inverse0, inverse1, inverse2, inverse3):
    target = (elem_owner[:, 0] * LEAF + elem_row).astype(jnp.int32)
    loads = jnp.zeros((NRHS, LEAF * DEVICES), jnp.float32).at[:, target].add(elem_loads)
    blocks = leaf_inverse.reshape(DEVICES, LEAF, LEAF)
    leaf_y = jnp.einsum("cdj,dij->cdi", loads.reshape(NRHS, DEVICES, LEAF), blocks, precision=HIGH).reshape(NRHS, -1)
    inverses = [inverse0, inverse1, inverse2, inverse3]
    couplings = [coupling0, coupling1, coupling2, leaf_coupling]
    sep_y = [None] * 4
    child = leaf_y
    for level in (3, 2, 1, 0):
        groups = 2 ** level
        width = SR * DEVICES // groups
        mat = couplings[level].reshape(width, groups, -1)
        term = jnp.einsum("sgj,cgj->cgs", mat, child.reshape(NRHS, groups, -1), precision=HIGH)
        resid = sep_loads[level].reshape(NRHS, groups, width) - term
        square = inverses[level].reshape(groups, width, width)
        sep_y[level] = jnp.einsum("gij,cgj->cgi", square, resid, precision=HIGH).reshape(NRHS, -1)
        child = sep_y[level]
    solved = []
    parent = None
    for level in range(4):
        groups = 2 ** level
        width = SR * DEVICES // groups
        upper = sep_y[level]
        if level > 0:
            pwidth = width * 2
            mat = couplings[level - 1].reshape(pwidth, groups // 2, -1)
            corr = jnp.einsum("sgj,cgs->cgj", mat, parent.reshape(NRHS, groups // 2, pwidth), precision=HIGH)
            upper = upper - corr.reshape(NRHS, -1)
        square = inverses[level].reshape(groups, width, width)
        parent = jnp.einsum("gij,cgi->cgj", square, upper.reshape(NRHS, groups, width), precision=HIGH).reshape(NRHS, -1)
        solved.append(parent)
    mat = leaf_coupling.reshape(SEP3, 8, -1)
    corr = jnp.einsum("sgj,cgs->cgj", mat, parent.reshape(NRHS, 8, SEP3), precision=HIGH).reshape(NRHS, -1)
    upper = (leaf_y - corr).reshape(NRHS, DEVICES, LEAF)
    leaf_solution = jnp.einsum("dij,cdi->cdj", blocks, upper, precision=HIGH).reshape(NRHS, -1)
    return leaf_solution, jnp.stack(solved)
```

```python
import functools
import jax
import jax.numpy as jnp
from jax import lax
from jax.experimental import pallas as pl
from jax.experimental.pallas import tpu as pltpu
from jax.sharding import PartitionSpec as P

F32 = jnp.float32
BF16 = jnp.bfloat16
AXES = ("cube", "front")
MESH = pl.DeviceIdType.MESH

NN = ((1,), (0,))
NT = ((1,), (1,))
TN = ((0,), (0,))


def raw(a, b, dims):
    return lax.dot_general(a, b, (dims, ((), ())), preferred_element_type=F32)


def split(x):
    high = x.astype(BF16)
    return high, (x - high.astype(F32)).astype(BF16)


def mm_split(a, high, low, dims):
    a_high, a_low = split(a)
    rows = a.shape[0]
    both = raw(jnp.concatenate([a_high, a_low], 0), high, dims)
    return both[:rows] + both[rows:] + raw(a_high, low, dims)


def mm(a, b, dims):
    high, low = split(b)
    return mm_split(a, high, low, dims)


def iota(shape, dim):
    return lax.broadcasted_iota(jnp.int32, shape, dim)


def kernel(
    devices, front, sr, sizes, cap, half,
    vals, owner, rows, w1, w2, w3, inv0, inv0_blocks, leaf_inv, leaf_coup,
    leaf_out, sep_out,
    linv, lhigh, llow, sendv, sendi, recvv, recvi, g1, g2, g3, blocks, inv0_other,
    x3, x2, x1, x0, x2s, x1s, x0s, hs, hg, y0,
    lsem, vs, vr, is_, ir, g1s, g1r, g2s, g2r, g3s, g3r, bs, br, hss, hsr, ys, yr, x3ss, x3r, ps, pr,
):
    n0, n1, n2, n3 = sizes
    me = lax.axis_index("cube") * front + lax.axis_index("front")
    m1, m2, m3 = devices // 2, devices // 4, devices // 8
    nrhs = vals.shape[0]
    leaf = leaf_coup.shape[1]
    elems = vals.shape[1]

    def dev(p):
        return (p // front, p % front)

    def partner(bit):
        return me + bit * (1 - 2 * ((me // bit) % 2))

    def remote(src, dst, ssem, rsem, p):
        return pltpu.make_async_remote_copy(
            src_ref=src, dst_ref=dst, send_sem=ssem, recv_sem=rsem,
            device_id=dev(p), device_id_type=MESH)

    fetch = pltpu.make_async_copy(leaf_inv, linv, lsem.at[0])
    fetch.start()

    barrier = pltpu.get_barrier_semaphore()

    def greet(j, _):
        pl.semaphore_signal(barrier, inc=1, device_id=dev((me + j) % devices), device_id_type=MESH)
        return 0

    lax.fori_loop(1, devices, greet, 0)

    own = owner[...]
    marks = iota((devices, elems), 0) == own
    marks_f = jnp.where(marks, 1.0, 0.0).astype(F32)
    earlier = jnp.where(iota((elems, elems), 0) < iota((elems, elems), 1), 1.0, 0.0).astype(BF16)
    before = raw(marks_f.astype(BF16), earlier, NN)
    rank = jnp.sum(before * marks_f, axis=0, keepdims=True).astype(jnp.int32)
    v = vals[...]
    v_a = v.astype(BF16)
    rest = v - v_a.astype(F32)
    v_b = rest.astype(BF16)
    v_c = (rest - v_b.astype(F32)).astype(BF16)
    place = iota((devices * half, elems), 0)
    sides = []
    for side in range(2):
        low = side * half
        target = jnp.where((rank >= low) & (rank < low + half), own * half + rank - low, -1)
        hot = jnp.where(place == target, 1.0, 0.0).astype(BF16)
        sides.append(raw(hot, v_a, NT) + raw(hot, v_b, NT) + raw(hot, v_c, NT))
    sendv[...] = jnp.concatenate(sides, 1).reshape(sendv.shape)
    number = rows[...].astype(F32)
    upper = jnp.floor(number * 0.0078125)
    lower = number - upper * 128.0
    ranks = jnp.where(iota((128, elems), 0) == rank, 1.0, 0.0).astype(BF16)
    sendi[...] = (
        raw((marks_f * upper).astype(BF16), ranks, NT) * 128.0
        + raw((marks_f * lower).astype(BF16), ranks, NT)
    ).reshape(sendi.shape)
    recvv[me] = sendv[me]
    recvi[me] = sendi[me]

    pl.semaphore_wait(barrier, devices - 1)

    def load_copies(p, slot, sem):
        return (
            remote(sendv.at[p], recvv.at[slot], vs.at[p], vr.at[sem], p),
            remote(sendi.at[p], recvi.at[slot], is_.at[p], ir.at[sem], p),
        )

    def send_loads(j, _):
        for copy in load_copies((me + j) % devices, me, me):
            copy.start()
        return 0

    lax.fori_loop(1, devices, send_loads, 0)

    def group_copy(src, dst, ssem, rsem, size, j, arriving):
        p = me // size * size + (me + j) % size
        slot = p % size if arriving else me % size
        return remote(src, dst.at[slot], ssem.at[p % size], rsem.at[slot], p)

    def group(src, dst, ssem, rsem, size, act):
        def body(j, _):
            copy = group_copy(src, dst, ssem, rsem, size, j, act != "start")
            if act == "start":
                copy.start()
            elif act == "recv":
                copy.wait_recv()
            else:
                copy.wait_send()
            return 0
        lax.fori_loop(1, size, body, 0)

    other0 = partner(m1)
    inv0_copy = remote(inv0, inv0_other, ps.at[0], pr.at[0], other0)

    group(w3, g3, g3s, g3r, m3, "start")
    group(w2, g2, g2s, g2r, m2, "start")
    inv0_copy.start()
    group(w1, g1, g1s, g1r, m1, "start")

    def block_copy(j, arriving):
        p = (me + j) % devices
        slot = p if arriving else me
        return remote(inv0_blocks.at[p], blocks.at[slot], bs.at[p], br.at[slot], p)

    def send_block(j, _):
        block_copy(j, False).start()
        return 0

    lax.fori_loop(1, devices, send_block, 0)
    g1[me % m1] = w1[...]
    g2[me % m2] = w2[...]
    g3[me % m3] = w3[...]
    blocks[me] = inv0_blocks[me]

    fetch.wait()
    linv_value = linv[...]
    high = linv_value.astype(BF16)
    lhigh[...] = high
    llow[...] = (linv_value - high.astype(F32)).astype(BF16)

    def get_loads(j, _):
        p = (me + j) % devices
        for copy in load_copies(p, p, p):
            copy.wait_recv()
        return 0

    lax.fori_loop(1, devices, get_loads, 0)

    slots = devices * half
    arrived = jnp.transpose(recvv[...].reshape(slots, 128))
    pick = jnp.where(iota((slots, devices), 0) // half == iota((slots, devices), 1), 1.0, 0.0).astype(BF16)
    ids = recvi[...].reshape(devices, 128)
    ids_up = jnp.floor(ids * 0.0078125)
    ids_low = ids - ids_up * 128.0
    spread = raw(pick, ids_up.astype(BF16), NN) * 128.0 + raw(pick, ids_low.astype(BF16), NN)
    lane = iota((slots, 128), 1)
    turn = iota((slots, 128), 0) % half
    loads = None
    for side in range(2):
        row = jnp.sum(jnp.where(lane == turn + side * half, spread, 0.0), axis=1, keepdims=True)
        hot = jnp.where(iota((slots, leaf), 1) == row.astype(jnp.int32), 1.0, 0.0).astype(BF16)
        part_high, part_low = split(arrived[side * nrhs:(side + 1) * nrhs])
        both = raw(jnp.concatenate([part_high, part_low], 0), hot, NN)
        term = both[:nrhs] + both[nrhs:]
        loads = term if loads is None else loads + term
    leaf_y = mm_split(loads, lhigh[...], llow[...], NT)
    coup = leaf_coup[...]
    x3[me % m3] = mm(leaf_y, coup, NT)
    group(x3.at[me % m3], x3, x3ss, x3r, m3, "start")

    group(w3, g3, g3s, g3r, m3, "recv")
    group(w2, g2, g2s, g2r, m2, "recv")
    c2t = g3[:, :, :n2].reshape(m3 * sr, n2)
    inv3 = g3[:, :, n2:n2 + n3].reshape(m3 * sr, n3)
    s3 = jnp.transpose(g3[:, :, n2 + n3:].reshape(m3 * sr, nrhs))
    c1t = g2[:, :, :n1].reshape(m2 * sr, n1)
    inv2 = g2[:, :, n1:n1 + n2].reshape(m2 * sr, n2)
    s2 = jnp.transpose(g2[:, :, n1 + n2:n1 + n2 + nrhs].reshape(m2 * sr, nrhs))


    def get_x3(j, _):
        p = me // m3 * m3 + (me + j) % m3
        remote(x3.at[me % m3], x3.at[p % m3], x3ss.at[p % m3], x3r.at[p % m3], p).wait_recv()
        return 0

    lax.fori_loop(1, m3, get_x3, 0)
    y3 = mm(s3 - jnp.sum(x3[...], axis=0), inv3, NT)
    t2 = mm(y3, c2t, NN)
    x2s[...] = t2
    copy2 = remote(x2s, x2, ps.at[1], pr.at[1], partner(m3))
    copy2.start()

    group(w1, g1, g1s, g1r, m1, "recv")
    inv0_copy.wait_recv()
    c0t = g1[:, :, :n0].reshape(m1 * sr, n0)
    pair0 = jnp.concatenate([inv0[...], inv0_other[...]], 0)
    hmat = mm(pair0, c0t, NT)
    hs[...] = hmat
    hg[me % m1] = hmat
    group(hs, hg, hss, hsr, m1, "start")

    copy2.wait_recv()
    y2 = mm(s2 - t2 - x2[...], inv2, NT)
    t1 = mm(y2, c1t, NN)
    x1s[...] = t1
    copy1 = remote(x1s, x1, ps.at[2], pr.at[2], partner(m2))
    copy1.start()

    inv1 = g1[:, :, n0:n0 + n1].reshape(m1 * sr, n1)
    s01 = g1[:, :, n0 + n1:].reshape(m1 * sr, 2 * nrhs)
    s1 = jnp.transpose(s01[:, nrhs:])
    second = me // m1 == 1
    mine0 = jnp.where(second, pair0[:, n1:], pair0[:, :n1])
    base = mm(mine0, s01[:, :nrhs], NN)

    copy1.wait_recv()
    y1 = mm(s1 - t1 - x1[...], inv1, NT)
    part = base - mm(hmat, y1, NT)
    eight = sr // 2
    x0s[...] = jnp.concatenate([part[sr:sr + eight], part[sr + eight:]], 1)
    copy0 = remote(x0s, x0, ps.at[3], pr.at[3], other0)
    copy0.start()
    copy0.wait_recv()
    y0[me] = jnp.concatenate([part[:eight], part[eight:sr]], 1) + x0[...]

    def y_copy(j, arriving):
        p = (me + j) % devices
        slot = p if arriving else me
        return remote(y0.at[me], y0.at[slot], ys.at[p], yr.at[slot], p)

    def send_y(j, _):
        y_copy(j, False).start()
        return 0

    lax.fori_loop(1, devices, send_y, 0)
    group(hs, hg, hss, hsr, m1, "recv")

    def get_block(j, _):
        block_copy(j, True).wait_recv()
        return 0

    lax.fori_loop(1, devices, get_block, 0)

    def get_y(j, _):
        y_copy(j, True).wait_recv()
        return 0

    lax.fori_loop(1, devices, get_y, 0)

    z1 = y1
    for far in range(2):
        where_ = (me // m1 + far) % 2 * m1
        turned = jnp.transpose(y0[pl.ds(where_, m1)].reshape(m1 * eight, 2 * nrhs))
        for side in range(2):
            piece = hg[:, far * sr + side * eight:far * sr + (side + 1) * eight, :].reshape(m1 * eight, n1)
            z1 = z1 - mm(turned[side * nrhs:(side + 1) * nrhs], piece, NN)

    sol1 = mm(z1, inv1, NN)
    sol2 = mm(y2 - mm(sol1, c1t, NT), inv2, NN)
    sol3 = mm(y3 - mm(sol2, c2t, NT), inv3, NN)
    leaf_out[...] = mm_split(leaf_y - mm(sol3, coup, NN), lhigh[...], llow[...], NN)

    full = jnp.transpose(y0[...].reshape(devices * eight, 2 * nrhs))
    sol0 = None
    for side in range(2):
        piece = blocks[:, side * eight:(side + 1) * eight, :].reshape(devices * eight, sr)
        term = mm(full[side * nrhs:(side + 1) * nrhs], piece, NN)
        sol0 = term if sol0 is None else sol0 + term
    sep_out[0] = sol0
    for level, value, size in ((1, sol1, m1), (2, sol2, m2), (3, sol3, m3)):
        wide = value.shape[1]
        chosen = jnp.where(iota((wide, sr), 0) == me % size * sr + iota((wide, sr), 1), 1.0, 0.0).astype(BF16)
        a = value.astype(BF16)
        left = value - a.astype(F32)
        b = left.astype(BF16)
        c = (left - b.astype(F32)).astype(BF16)
        sep_out[level] = raw(a, chosen, NN) + raw(b, chosen, NN) + raw(c, chosen, NN)

    def sent(j, _):
        p = (me + j) % devices
        for copy in load_copies(p, me, me):
            copy.wait_send()
        block_copy(j, False).wait_send()
        y_copy(j, False).wait_send()
        return 0

    lax.fori_loop(1, devices, sent, 0)
    group(w3, g3, g3s, g3r, m3, "sent")
    group(w2, g2, g2s, g2r, m2, "sent")
    group(w1, g1, g1s, g1r, m1, "sent")
    group(hs, hg, hss, hsr, m1, "sent")

    def sent_x3(j, _):
        p = me // m3 * m3 + (me + j) % m3
        remote(x3.at[me % m3], x3.at[me % m3], x3ss.at[p % m3], x3r.at[me % m3], p).wait_send()
        return 0

    lax.fori_loop(1, m3, sent_x3, 0)
    for copy in (inv0_copy, copy2, copy1, copy0):
        copy.wait_send()


def shards(
    elem_loads, elem_owner, elem_row, sep_loads, leaf_inverse, leaf_coupling,
    coupling0, coupling1, coupling2, inverse0, inverse1, inverse2, inverse3,
):
    front = lax.axis_size("front")
    devices = lax.axis_size(AXES)
    nrhs, elems = elem_loads.shape
    leaf = leaf_inverse.shape[0]
    sr = sep_loads.shape[2]
    sizes = (inverse0.shape[1], inverse1.shape[1], inverse2.shape[1], inverse3.shape[1])
    n0, n1, n2, n3 = sizes
    cap = 2 * elems // devices
    half = max(8, -(-cap // 16) * 8)
    m1, m2, m3 = devices // 2, devices // 4, devices // 8
    turned = jnp.transpose(sep_loads, (2, 0, 1))
    w1 = jnp.concatenate([coupling0.T, inverse1, turned[:, 0], turned[:, 1]], 1)
    w2 = jnp.concatenate([coupling1.T, inverse2, turned[:, 2], turned[:, 2]], 1)
    w3 = jnp.concatenate([coupling2.T, inverse3, turned[:, 3]], 1)
    blocks = jnp.transpose(inverse0.reshape(sr, devices, sr), (1, 0, 2))
    vmem = pl.BlockSpec(memory_space=pltpu.VMEM)
    dma = pltpu.SemaphoreType.DMA
    V = pltpu.VMEM
    return tuple(pl.pallas_call(
        functools.partial(kernel, devices, front, sr, sizes, cap, half),
        out_shape=(
            jax.ShapeDtypeStruct((nrhs, leaf), F32),
            jax.ShapeDtypeStruct(sep_loads.shape, F32),
        ),
        in_specs=[vmem] * 8 + [pl.BlockSpec(memory_space=pl.ANY), vmem],
        out_specs=(vmem, vmem),
        scratch_shapes=[
            V((leaf, leaf), F32), V((leaf, leaf), BF16), V((leaf, leaf), BF16),
            V((devices, half, 2 * nrhs), F32), V((devices, 1, 128), F32),
            V((devices, half, 2 * nrhs), F32), V((devices, 1, 128), F32),
            V((m1, *w1.shape), F32), V((m2, *w2.shape), F32), V((m3, *w3.shape), F32),
            V((devices, sr, sr), F32), V((sr, n0), F32),
            V((m3, nrhs, n3), F32), V((nrhs, n2), F32), V((nrhs, n1), F32), V((sr // 2, 2 * nrhs), F32),
            V((nrhs, n2), F32), V((nrhs, n1), F32), V((sr // 2, 2 * nrhs), F32),
            V((2 * sr, n1), F32), V((m1, 2 * sr, n1), F32), V((devices, sr // 2, 2 * nrhs), F32),
            dma((1,)), dma((devices,)), dma((devices,)), dma((devices,)), dma((devices,)),
            dma((m1,)), dma((m1,)), dma((m2,)), dma((m2,)), dma((m3,)), dma((m3,)),
            dma((devices,)), dma((devices,)), dma((m1,)), dma((m1,)), dma((devices,)), dma((devices,)),
            dma((m3,)), dma((m3,)), dma((4,)), dma((4,)),
        ],
        compiler_params=pltpu.CompilerParams(
            collective_id=0, has_side_effects=True, vmem_limit_bytes=60 * 1024 * 1024),
    )(elem_loads, elem_owner.reshape(1, elems), elem_row.reshape(1, elems), w1, w2, w3,
      inverse0, blocks, leaf_inverse, leaf_coupling))


def solution(mesh):
    in_specs = (
        P(None, AXES), P(AXES, None), P(AXES), P(None, None, AXES), P(AXES, None), P(None, AXES),
        P(None, AXES), P(None, AXES), P(None, AXES),
        P(AXES, None), P(AXES, None), P(AXES, None), P(AXES, None),
    )
    out_specs = (P(None, AXES), P(None, None, AXES))
    return jax.shard_map(shards, mesh=mesh, in_specs=in_specs, out_specs=out_specs, check_vma=False)
```

```python
import functools
import jax
import jax.numpy as jnp
from jax import lax
from jax.experimental import pallas as pl
from jax.experimental.pallas import tpu as pltpu
from jax.sharding import PartitionSpec as P

F32 = jnp.float32
BF16 = jnp.bfloat16
AXES = ("cube", "front")
MESH = pl.DeviceIdType.MESH

NN = ((1,), (0,))
NT = ((1,), (1,))
TN = ((0,), (0,))


def raw(a, b, dims):
    return lax.dot_general(a, b, (dims, ((), ())), preferred_element_type=F32)


def split(x):
    high = x.astype(BF16)
    return high, (x - high.astype(F32)).astype(BF16)


def mm_split(a, high, low, dims):
    a_high, a_low = split(a)
    rows = a.shape[0]
    both = raw(jnp.concatenate([a_high, a_low], 0), high, dims)
    return both[:rows] + both[rows:] + raw(a_high, low, dims)


def mm(a, b, dims):
    high, low = split(b)
    return mm_split(a, high, low, dims)


def iota(shape, dim):
    return lax.broadcasted_iota(jnp.int32, shape, dim)


def kernel(
    devices, front, sr, sizes, cap, half,
    vals, owner, rows, sep, inv0, inv1_own, inv2_own, inv3_own, coup0, coup1, coup2, leaf_inv, leaf_coup,
    leaf_out, sep_out,
    linv, lhigh, llow, sendv, sendi, recvv, recvi, g1, g2, g3, inv0_blocks, blocks, inv0_other,
    x3, x2, x1, x0, x2s, x1s, x0s, hg, y0,
    lsem, vs, vr, is_, ir, g1s, g1r, g2s, g2r, g3s, g3r, bs, br, hss, hsr, ys, yr, x3ss, x3r, ps, pr, g1f, hf,
):
    n0, n1, n2, n3 = sizes
    me = lax.axis_index("cube") * front + lax.axis_index("front")
    m1, m2, m3 = devices // 2, devices // 4, devices // 8
    nrhs = vals.shape[0]
    leaf = leaf_coup.shape[1]
    elems = vals.shape[1]

    def dev(p):
        return (p // front, p % front)

    def partner(bit):
        return me + bit * (1 - 2 * ((me // bit) % 2))

    def remote(src, dst, ssem, rsem, p):
        return pltpu.make_async_remote_copy(
            src_ref=src, dst_ref=dst, send_sem=ssem, recv_sem=rsem,
            device_id=dev(p), device_id_type=MESH)

    fetch = pltpu.make_async_copy(leaf_inv, linv, lsem.at[0])
    fetch.start()

    barrier = pltpu.get_barrier_semaphore()

    def greet(j, _):
        pl.semaphore_signal(barrier, inc=1, device_id=dev((me + j) % devices), device_id_type=MESH)
        return 0

    lax.fori_loop(1, devices, greet, 0)

    eye = iota((elems, elems), 0) == iota((elems, elems), 1)
    own = jnp.sum(jnp.where(eye, owner[...], 0), axis=0, keepdims=True)
    marks = iota((devices, elems), 0) == own
    marks_f = jnp.where(marks, 1.0, 0.0).astype(F32)
    earlier = jnp.where(iota((elems, elems), 0) < iota((elems, elems), 1), 1.0, 0.0).astype(BF16)
    before = raw(marks_f.astype(BF16), earlier, NN)
    rank = jnp.sum(before * marks_f, axis=0, keepdims=True).astype(jnp.int32)
    v = vals[...]
    v_a = v.astype(BF16)
    rest = v - v_a.astype(F32)
    v_b = rest.astype(BF16)
    v_c = (rest - v_b.astype(F32)).astype(BF16)
    place = iota((devices * half, elems), 0)
    sides = []
    for side in range(2):
        low = side * half
        target = jnp.where((rank >= low) & (rank < low + half), own * half + rank - low, -1)
        hot = jnp.where(place == target, 1.0, 0.0).astype(BF16)
        sides.append(raw(hot, v_a, NT) + raw(hot, v_b, NT) + raw(hot, v_c, NT))
    sendv[...] = jnp.concatenate(sides, 1).reshape(sendv.shape)
    number = rows[...].astype(F32)
    upper = jnp.floor(number * 0.0078125)
    lower = number - upper * 128.0
    ranks = jnp.where(iota((128, elems), 0) == rank, 1.0, 0.0).astype(BF16)
    sendi[...] = (
        raw((marks_f * upper).astype(BF16), ranks, NT) * 128.0
        + raw((marks_f * lower).astype(BF16), ranks, NT)
    ).reshape(sendi.shape)
    g1[me % m1] = jnp.concatenate(
        [jnp.transpose(coup0[...]), inv1_own[...], jnp.transpose(sep[0]), jnp.transpose(sep[1])], 1)
    own2 = jnp.transpose(sep[2])
    g2[me % m2] = jnp.concatenate([jnp.transpose(coup1[...]), inv2_own[...], own2, own2], 1)
    g3[me % m3] = jnp.concatenate([jnp.transpose(coup2[...]), inv3_own[...], jnp.transpose(sep[3])], 1)
    recvv[me] = sendv[me]
    recvi[me] = sendi[me]

    pl.semaphore_wait(barrier, devices - 1)

    def load_copies(p, slot, sem):
        return (
            remote(sendv.at[p], recvv.at[slot], vs.at[p], vr.at[sem], p),
            remote(sendi.at[p], recvi.at[slot], is_.at[p], ir.at[sem], p),
        )

    def send_loads(j, _):
        for copy in load_copies((me + j) % devices, me, me):
            copy.start()
        return 0

    lax.fori_loop(1, devices, send_loads, 0)

    def group_copy(src, dst, ssem, rsem, size, j, arriving):
        p = me // size * size + (me + j) % size
        slot = p % size if arriving else me % size
        return remote(src, dst.at[slot], ssem.at[p % size], rsem.at[slot], p)

    def group(src, dst, ssem, rsem, size, act):
        def body(j, _):
            copy = group_copy(src, dst, ssem, rsem, size, j, act != "start")
            if act == "start":
                copy.start()
            elif act == "recv":
                copy.wait_recv()
            else:
                copy.wait_send()
            return 0
        lax.fori_loop(1, size, body, 0)

    other0 = partner(m1)
    inv0_copy = remote(inv0, inv0_other, ps.at[0], pr.at[0], other0)

    group(g3.at[me % m3], g3, g3s, g3r, m3, "start")
    group(g2.at[me % m2], g2, g2s, g2r, m2, "start")
    inv0_copy.start()
    twin = partner(1)

    def wide(dst, ssem, rsem, fsem, act):
        start = me // m1 * m1

        def slot_of(first, j):
            return (first % m1 + front * j) % m1

        def direct(j, _):
            slot = slot_of(me, j)
            if act == "start":
                remote(dst.at[me % m1], dst.at[me % m1], ssem.at[slot], rsem.at[me % m1], start + slot).start()
            elif act == "sent":
                remote(dst.at[me % m1], dst.at[me % m1], ssem.at[slot], rsem.at[me % m1], start + slot).wait_send()
            elif act == "pass":
                remote(dst.at[slot], dst.at[slot], ssem.at[slot], rsem.at[slot], start + slot).wait_recv()
                remote(dst.at[slot], dst.at[slot], fsem.at[slot], rsem.at[slot], twin).start()
            return 0

        def passed(j, _):
            if act == "sent":
                slot = slot_of(me, j)
                remote(dst.at[slot], dst.at[slot], fsem.at[slot], rsem.at[slot], twin).wait_send()
            else:
                slot = slot_of(twin, j)
                remote(dst.at[slot], dst.at[slot], fsem.at[slot], rsem.at[slot], twin).wait_recv()
            return 0

        if act == "start":
            mine = me % m1
            remote(dst.at[mine], dst.at[mine], fsem.at[mine], rsem.at[mine], twin).start()
        if act != "recv":
            lax.fori_loop(1, m1 // front, direct, 0)
        if act in ("recv", "sent"):
            lax.fori_loop(0, m1 // front, passed, 0)

    wide(g1, g1s, g1r, g1f, "start")

    def block_copy(j, arriving):
        p = (me + j) % devices
        slot = p if arriving else me
        return remote(inv0_blocks.at[p], blocks.at[slot], bs.at[p], br.at[slot], p)

    def send_block(j, _):
        block_copy(j, False).start()
        return 0

    inv0_value = inv0[...]
    for p in range(devices):
        inv0_blocks[p] = inv0_value[:, p * sr:(p + 1) * sr]
    blocks[me] = inv0_blocks[me]

    fetch.wait()
    linv_value = linv[...]
    high = linv_value.astype(BF16)
    lhigh[...] = high
    llow[...] = (linv_value - high.astype(F32)).astype(BF16)

    def get_loads(j, _):
        p = (me + j) % devices
        for copy in load_copies(p, p, p):
            copy.wait_recv()
        return 0

    lax.fori_loop(1, devices, get_loads, 0)

    slots = devices * half
    arrived = jnp.transpose(recvv[...].reshape(slots, 128))
    pick = jnp.where(iota((slots, devices), 0) // half == iota((slots, devices), 1), 1.0, 0.0).astype(BF16)
    ids = recvi[...].reshape(devices, 128)
    ids_up = jnp.floor(ids * 0.0078125)
    ids_low = ids - ids_up * 128.0
    spread = raw(pick, ids_up.astype(BF16), NN) * 128.0 + raw(pick, ids_low.astype(BF16), NN)
    lane = iota((slots, 128), 1)
    turn = iota((slots, 128), 0) % half
    loads = None
    for side in range(2):
        row = jnp.sum(jnp.where(lane == turn + side * half, spread, 0.0), axis=1, keepdims=True)
        hot = jnp.where(iota((slots, leaf), 1) == row.astype(jnp.int32), 1.0, 0.0).astype(BF16)
        part_high, part_low = split(arrived[side * nrhs:(side + 1) * nrhs])
        both = raw(jnp.concatenate([part_high, part_low], 0), hot, NN)
        term = both[:nrhs] + both[nrhs:]
        loads = term if loads is None else loads + term
    leaf_y = mm_split(loads, lhigh[...], llow[...], NT)
    coup = leaf_coup[...]
    x3[me % m3] = mm(leaf_y, coup, NT)
    group(x3.at[me % m3], x3, x3ss, x3r, m3, "start")

    group(g3.at[me % m3], g3, g3s, g3r, m3, "recv")
    group(g2.at[me % m2], g2, g2s, g2r, m2, "recv")
    c2t = g3[:, :, :n2].reshape(m3 * sr, n2)
    inv3 = g3[:, :, n2:n2 + n3].reshape(m3 * sr, n3)
    s3 = jnp.transpose(g3[:, :, n2 + n3:].reshape(m3 * sr, nrhs))
    c1t = g2[:, :, :n1].reshape(m2 * sr, n1)
    inv2 = g2[:, :, n1:n1 + n2].reshape(m2 * sr, n2)
    s2 = jnp.transpose(g2[:, :, n1 + n2:n1 + n2 + nrhs].reshape(m2 * sr, nrhs))


    def get_x3(j, _):
        p = me // m3 * m3 + (me + j) % m3
        remote(x3.at[me % m3], x3.at[p % m3], x3ss.at[p % m3], x3r.at[p % m3], p).wait_recv()
        return 0

    lax.fori_loop(1, m3, get_x3, 0)
    y3 = mm(s3 - jnp.sum(x3[...], axis=0), inv3, NT)
    t2 = mm(y3, c2t, NN)
    x2s[...] = t2
    copy2 = remote(x2s, x2, ps.at[1], pr.at[1], partner(m3))
    copy2.start()

    wide(g1, g1s, g1r, g1f, "pass")

    copy2.wait_recv()
    y2 = mm(s2 - t2 - x2[...], inv2, NT)
    t1 = mm(y2, c1t, NN)
    x1s[...] = t1
    copy1 = remote(x1s, x1, ps.at[2], pr.at[2], partner(m2))
    copy1.start()

    wide(g1, g1s, g1r, g1f, "recv")
    inv0_copy.wait_recv()
    c0t = g1[:, :, :n0].reshape(m1 * sr, n0)
    pair0 = jnp.concatenate([inv0[...], inv0_other[...]], 0)
    hmat = mm(pair0, c0t, NT)
    hg[me % m1] = hmat
    wide(hg, hss, hsr, hf, "start")
    inv1 = g1[:, :, n0:n0 + n1].reshape(m1 * sr, n1)
    s01 = g1[:, :, n0 + n1:].reshape(m1 * sr, 2 * nrhs)
    s1 = jnp.transpose(s01[:, nrhs:])
    second = me // m1 == 1
    mine0 = jnp.where(second, pair0[:, n1:], pair0[:, :n1])
    base = mm(mine0, s01[:, :nrhs], NN)

    copy1.wait_recv()
    y1 = mm(s1 - t1 - x1[...], inv1, NT)
    part = base - mm(hmat, y1, NT)
    eight = sr // 2
    x0s[...] = jnp.concatenate([part[sr:sr + eight], part[sr + eight:]], 1)
    copy0 = remote(x0s, x0, ps.at[3], pr.at[3], other0)
    copy0.start()
    copy0.wait_recv()
    y0[me] = jnp.concatenate([part[:eight], part[eight:sr]], 1) + x0[...]

    def y_copy(j, arriving):
        p = (me + j) % devices
        slot = p if arriving else me
        return remote(y0.at[me], y0.at[slot], ys.at[p], yr.at[slot], p)

    def send_y(j, _):
        y_copy(j, False).start()
        return 0

    lax.fori_loop(1, devices, send_y, 0)
    wide(hg, hss, hsr, hf, "pass")
    lax.fori_loop(1, devices, send_block, 0)

    def get_block(j, _):
        block_copy(j, True).wait_recv()
        return 0

    def get_y(j, _):
        y_copy(j, True).wait_recv()
        return 0

    lax.fori_loop(1, devices, get_y, 0)
    wide(hg, hss, hsr, hf, "recv")

    z1 = y1
    for far in range(2):
        where_ = (me // m1 + far) % 2 * m1
        turned = jnp.transpose(y0[pl.ds(where_, m1)].reshape(m1 * eight, 2 * nrhs))
        for side in range(2):
            piece = hg[:, far * sr + side * eight:far * sr + (side + 1) * eight, :].reshape(m1 * eight, n1)
            z1 = z1 - mm(turned[side * nrhs:(side + 1) * nrhs], piece, NN)

    sol1 = mm(z1, inv1, NN)
    sol2 = mm(y2 - mm(sol1, c1t, NT), inv2, NN)
    sol3 = mm(y3 - mm(sol2, c2t, NT), inv3, NN)
    leaf_out[...] = mm_split(leaf_y - mm(sol3, coup, NN), lhigh[...], llow[...], NN)

    lax.fori_loop(1, devices, get_block, 0)
    full = jnp.transpose(y0[...].reshape(devices * eight, 2 * nrhs))
    sol0 = None
    for side in range(2):
        piece = blocks[:, side * eight:(side + 1) * eight, :].reshape(devices * eight, sr)
        term = mm(full[side * nrhs:(side + 1) * nrhs], piece, NN)
        sol0 = term if sol0 is None else sol0 + term
    sep_out[0] = sol0
    for level, value, size in ((1, sol1, m1), (2, sol2, m2), (3, sol3, m3)):
        width = value.shape[1]
        chosen = jnp.where(iota((width, sr), 0) == me % size * sr + iota((width, sr), 1), 1.0, 0.0).astype(BF16)
        a = value.astype(BF16)
        left = value - a.astype(F32)
        b = left.astype(BF16)
        c = (left - b.astype(F32)).astype(BF16)
        sep_out[level] = raw(a, chosen, NN) + raw(b, chosen, NN) + raw(c, chosen, NN)

    def sent(j, _):
        p = (me + j) % devices
        for copy in load_copies(p, me, me):
            copy.wait_send()
        block_copy(j, False).wait_send()
        y_copy(j, False).wait_send()
        return 0

    lax.fori_loop(1, devices, sent, 0)
    group(g3.at[me % m3], g3, g3s, g3r, m3, "sent")
    group(g2.at[me % m2], g2, g2s, g2r, m2, "sent")
    wide(g1, g1s, g1r, g1f, "sent")
    wide(hg, hss, hsr, hf, "sent")

    def sent_x3(j, _):
        p = me // m3 * m3 + (me + j) % m3
        remote(x3.at[me % m3], x3.at[me % m3], x3ss.at[p % m3], x3r.at[me % m3], p).wait_send()
        return 0

    lax.fori_loop(1, m3, sent_x3, 0)
    for copy in (inv0_copy, copy2, copy1, copy0):
        copy.wait_send()


def shards(
    elem_loads, elem_owner, elem_row, sep_loads, leaf_inverse, leaf_coupling,
    coupling0, coupling1, coupling2, inverse0, inverse1, inverse2, inverse3,
):
    front = lax.axis_size("front")
    devices = lax.axis_size(AXES)
    nrhs, elems = elem_loads.shape
    leaf = leaf_inverse.shape[0]
    sr = sep_loads.shape[2]
    sizes = (inverse0.shape[1], inverse1.shape[1], inverse2.shape[1], inverse3.shape[1])
    n0, n1, n2, n3 = sizes
    cap = 2 * elems // devices
    half = max(8, -(-cap // 16) * 8)
    m1, m2, m3 = devices // 2, devices // 4, devices // 8
    pad = 2 * nrhs
    vmem = pl.BlockSpec(memory_space=pltpu.VMEM)
    dma = pltpu.SemaphoreType.DMA
    V = pltpu.VMEM
    return tuple(pl.pallas_call(
        functools.partial(kernel, devices, front, sr, sizes, cap, half),
        out_shape=(
            jax.ShapeDtypeStruct((nrhs, leaf), F32),
            jax.ShapeDtypeStruct(sep_loads.shape, F32),
        ),
        in_specs=[vmem] * 11 + [pl.BlockSpec(memory_space=pl.ANY), vmem],
        out_specs=(vmem, vmem),
        scratch_shapes=[
            V((leaf, leaf), F32), V((leaf, leaf), BF16), V((leaf, leaf), BF16),
            V((devices, half, 2 * nrhs), F32), V((devices, 1, 128), F32),
            V((devices, half, 2 * nrhs), F32), V((devices, 1, 128), F32),
            V((m1, sr, n0 + n1 + pad), F32), V((m2, sr, n1 + n2 + pad), F32), V((m3, sr, n2 + n3 + nrhs), F32),
            V((devices, sr, sr), F32),
            V((devices, sr, sr), F32), V((sr, n0), F32),
            V((m3, nrhs, n3), F32), V((nrhs, n2), F32), V((nrhs, n1), F32), V((sr // 2, 2 * nrhs), F32),
            V((nrhs, n2), F32), V((nrhs, n1), F32), V((sr // 2, 2 * nrhs), F32),
            V((m1, 2 * sr, n1), F32), V((devices, sr // 2, 2 * nrhs), F32),
            dma((1,)), dma((devices,)), dma((devices,)), dma((devices,)), dma((devices,)),
            dma((m1,)), dma((m1,)), dma((m2,)), dma((m2,)), dma((m3,)), dma((m3,)),
            dma((devices,)), dma((devices,)), dma((m1,)), dma((m1,)), dma((devices,)), dma((devices,)),
            dma((m3,)), dma((m3,)), dma((4,)), dma((4,)), dma((m1,)), dma((m1,)),
        ],
        compiler_params=pltpu.CompilerParams(
            collective_id=0, has_side_effects=True, vmem_limit_bytes=60 * 1024 * 1024),
    )(elem_loads, elem_owner, elem_row.reshape(1, elems), sep_loads,
      inverse0, inverse1, inverse2, inverse3, coupling0, coupling1, coupling2,
      leaf_inverse, leaf_coupling))


def solution(mesh):
    in_specs = (
        P(None, AXES), P(AXES, None), P(AXES), P(None, None, AXES), P(AXES, None), P(None, AXES),
        P(None, AXES), P(None, AXES), P(None, AXES),
        P(AXES, None), P(AXES, None), P(AXES, None), P(AXES, None),
    )
    out_specs = (P(None, AXES), P(None, None, AXES))
    return jax.shard_map(shards, mesh=mesh, in_specs=in_specs, out_specs=out_specs, check_vma=False)
```

```python
import functools
import jax
import jax.numpy as jnp
from jax import lax
from jax.experimental import pallas as pl
from jax.experimental.pallas import tpu as pltpu
from jax.sharding import PartitionSpec as P

F32 = jnp.float32
BF16 = jnp.bfloat16
AXES = ("cube", "front")
MESH = pl.DeviceIdType.MESH

NN = ((1,), (0,))
NT = ((1,), (1,))
TN = ((0,), (0,))


def raw(a, b, dims):
    return lax.dot_general(a, b, (dims, ((), ())), preferred_element_type=F32)


def split(x):
    high = x.astype(BF16)
    return high, (x - high.astype(F32)).astype(BF16)


def mm_split(a, high, low, dims):
    a_high, a_low = split(a)
    rows = a.shape[0]
    both = raw(jnp.concatenate([a_high, a_low], 0), high, dims)
    return both[:rows] + both[rows:] + raw(a_high, low, dims)


def mm(a, b, dims):
    high, low = split(b)
    return mm_split(a, high, low, dims)


def iota(shape, dim):
    return lax.broadcasted_iota(jnp.int32, shape, dim)


def kernel(
    devices, front, sr, sizes, cap, half,
    vals, owner, rows, sep, inv0, inv1_own, inv2_own, inv3_own, coup0, coup1, coup2, leaf_inv, leaf_coup,
    leaf_out, sep_out,
    linv, lhigh, llow, sendv, sendi, recvv, recvi, g1, g2, g3, inv0_blocks, blocks, inv0_other,
    x3, x2, x1, x0, x2s, x1s, x0s, hg, y0,
    lsem, vs, vr, is_, ir, g1s, g1r, g2s, g2r, g3s, g3r, bs, br, hss, hsr, ys, yr, x3ss, x3r, ps, pr, g1f, hf,
):
    n0, n1, n2, n3 = sizes
    me = lax.axis_index("cube") * front + lax.axis_index("front")
    m1, m2, m3 = devices // 2, devices // 4, devices // 8
    nrhs = vals.shape[0]
    leaf = leaf_coup.shape[1]
    elems = vals.shape[1]

    def dev(p):
        return (p // front, p % front)

    def partner(bit):
        return me + bit * (1 - 2 * ((me // bit) % 2))

    def remote(src, dst, ssem, rsem, p):
        return pltpu.make_async_remote_copy(
            src_ref=src, dst_ref=dst, send_sem=ssem, recv_sem=rsem,
            device_id=dev(p), device_id_type=MESH)

    fetch = pltpu.make_async_copy(leaf_inv, linv, lsem.at[0])
    fetch.start()

    barrier = pltpu.get_barrier_semaphore()

    def greet(j, _):
        pl.semaphore_signal(barrier, inc=1, device_id=dev((me + j) % devices), device_id_type=MESH)
        return 0

    lax.fori_loop(1, devices, greet, 0)

    own = owner[...]
    marks = iota((devices, elems), 0) == own
    marks_f = jnp.where(marks, 1.0, 0.0).astype(F32)
    earlier = jnp.where(iota((elems, elems), 0) < iota((elems, elems), 1), 1.0, 0.0).astype(BF16)
    before = raw(marks_f.astype(BF16), earlier, NN)
    rank = jnp.sum(before * marks_f, axis=0, keepdims=True).astype(jnp.int32)
    v = vals[...]
    v_a = v.astype(BF16)
    rest = v - v_a.astype(F32)
    v_b = rest.astype(BF16)
    v_c = (rest - v_b.astype(F32)).astype(BF16)
    place = iota((devices * half, elems), 0)
    sides = []
    for side in range(2):
        low = side * half
        target = jnp.where((rank >= low) & (rank < low + half), own * half + rank - low, -1)
        hot = jnp.where(place == target, 1.0, 0.0).astype(BF16)
        sides.append(raw(hot, v_a, NT) + raw(hot, v_b, NT) + raw(hot, v_c, NT))
    sendv[...] = jnp.concatenate(sides, 1).reshape(sendv.shape)
    number = rows[...].astype(F32)
    upper = jnp.floor(number * 0.0078125)
    lower = number - upper * 128.0
    ranks = jnp.where(iota((128, elems), 0) == rank, 1.0, 0.0).astype(BF16)
    sendi[...] = (
        raw((marks_f * upper).astype(BF16), ranks, NT) * 128.0
        + raw((marks_f * lower).astype(BF16), ranks, NT)
    ).reshape(sendi.shape)
    g1[me % m1] = jnp.concatenate(
        [coup0[...], inv1_own[...], sep[0], sep[1]], 1)
    g2[me % m2] = jnp.concatenate([coup1[...], inv2_own[...], sep[2], sep[2]], 1)
    g3[me % m3] = jnp.concatenate([coup2[...], inv3_own[...], sep[3]], 1)
    recvv[me] = sendv[me]
    recvi[me] = sendi[me]

    pl.semaphore_wait(barrier, devices - 1)

    def load_copies(p, slot, sem):
        return (
            remote(sendv.at[p], recvv.at[slot], vs.at[p], vr.at[sem], p),
            remote(sendi.at[p], recvi.at[slot], is_.at[p], ir.at[sem], p),
        )

    def send_loads(j, _):
        for copy in load_copies((me + j) % devices, me, me):
            copy.start()
        return 0

    lax.fori_loop(1, devices, send_loads, 0)

    def group_copy(src, dst, ssem, rsem, size, j, arriving):
        p = me // size * size + (me + j) % size
        slot = p % size if arriving else me % size
        return remote(src, dst.at[slot], ssem.at[p % size], rsem.at[slot], p)

    def group(src, dst, ssem, rsem, size, act):
        def body(j, _):
            copy = group_copy(src, dst, ssem, rsem, size, j, act != "start")
            if act == "start":
                copy.start()
            elif act == "recv":
                copy.wait_recv()
            else:
                copy.wait_send()
            return 0
        lax.fori_loop(1, size, body, 0)

    other0 = partner(m1)
    inv0_copy = remote(inv0, inv0_other, ps.at[0], pr.at[0], other0)

    group(g3.at[me % m3], g3, g3s, g3r, m3, "start")
    group(g2.at[me % m2], g2, g2s, g2r, m2, "start")
    inv0_copy.start()
    twin = partner(1)

    def wide(dst, ssem, rsem, fsem, act):
        start = me // m1 * m1

        def slot_of(first, j):
            return (first % m1 + front * j) % m1

        def direct(j, _):
            slot = slot_of(me, j)
            if act == "start":
                remote(dst.at[me % m1], dst.at[me % m1], ssem.at[slot], rsem.at[me % m1], start + slot).start()
            elif act == "sent":
                remote(dst.at[me % m1], dst.at[me % m1], ssem.at[slot], rsem.at[me % m1], start + slot).wait_send()
            elif act == "pass":
                remote(dst.at[slot], dst.at[slot], ssem.at[slot], rsem.at[slot], start + slot).wait_recv()
                remote(dst.at[slot], dst.at[slot], fsem.at[slot], rsem.at[slot], twin).start()
            return 0

        def passed(j, _):
            if act == "sent":
                slot = slot_of(me, j)
                remote(dst.at[slot], dst.at[slot], fsem.at[slot], rsem.at[slot], twin).wait_send()
            else:
                slot = slot_of(twin, j)
                remote(dst.at[slot], dst.at[slot], fsem.at[slot], rsem.at[slot], twin).wait_recv()
            return 0

        if act == "start":
            mine = me % m1
            remote(dst.at[mine], dst.at[mine], fsem.at[mine], rsem.at[mine], twin).start()
        if act != "recv":
            lax.fori_loop(1, m1 // front, direct, 0)
        if act in ("recv", "sent"):
            lax.fori_loop(0, m1 // front, passed, 0)

    wide(g1, g1s, g1r, g1f, "start")

    def block_copy(j, arriving):
        p = (me + j) % devices
        slot = p if arriving else me
        return remote(inv0_blocks.at[p], blocks.at[slot], bs.at[p], br.at[slot], p)

    def send_block(j, _):
        block_copy(j, False).start()
        return 0

    inv0_value = inv0[...]
    for p in range(devices):
        inv0_blocks[p] = inv0_value[:, p * sr:(p + 1) * sr]
    blocks[me] = inv0_blocks[me]

    fetch.wait()
    linv_value = linv[...]
    high = linv_value.astype(BF16)
    lhigh[...] = high
    llow[...] = (linv_value - high.astype(F32)).astype(BF16)

    def get_loads(j, _):
        p = (me + j) % devices
        for copy in load_copies(p, p, p):
            copy.wait_recv()
        return 0

    lax.fori_loop(1, devices, get_loads, 0)

    slots = devices * half
    arrived = jnp.transpose(recvv[...].reshape(slots, 128))
    pick = jnp.where(iota((slots, devices), 0) // half == iota((slots, devices), 1), 1.0, 0.0).astype(BF16)
    ids = recvi[...].reshape(devices, 128)
    ids_up = jnp.floor(ids * 0.0078125)
    ids_low = ids - ids_up * 128.0
    spread = raw(pick, ids_up.astype(BF16), NN) * 128.0 + raw(pick, ids_low.astype(BF16), NN)
    lane = iota((slots, 128), 1)
    turn = iota((slots, 128), 0) % half
    loads = None
    for side in range(2):
        row = jnp.sum(jnp.where(lane == turn + side * half, spread, 0.0), axis=1, keepdims=True)
        hot = jnp.where(iota((slots, leaf), 1) == row.astype(jnp.int32), 1.0, 0.0).astype(BF16)
        part_high, part_low = split(arrived[side * nrhs:(side + 1) * nrhs])
        both = raw(jnp.concatenate([part_high, part_low], 0), hot, NN)
        term = both[:nrhs] + both[nrhs:]
        loads = term if loads is None else loads + term
    leaf_y = mm_split(loads, lhigh[...], llow[...], NT)
    coup = leaf_coup[...]
    x3[me % m3] = mm(leaf_y, coup, NT)
    group(x3.at[me % m3], x3, x3ss, x3r, m3, "start")

    group(g3.at[me % m3], g3, g3s, g3r, m3, "recv")
    group(g2.at[me % m2], g2, g2s, g2r, m2, "recv")
    c2t = g3[:, :, :n2].reshape(m3 * sr, n2)
    inv3 = g3[:, :, n2:n2 + n3].reshape(m3 * sr, n3)
    s3 = jnp.transpose(g3[:, :, n2 + n3:].reshape(m3 * sr, nrhs))
    c1t = g2[:, :, :n1].reshape(m2 * sr, n1)
    inv2 = g2[:, :, n1:n1 + n2].reshape(m2 * sr, n2)
    s2 = jnp.transpose(g2[:, :, n1 + n2:n1 + n2 + nrhs].reshape(m2 * sr, nrhs))


    def get_x3(j, _):
        p = me // m3 * m3 + (me + j) % m3
        remote(x3.at[me % m3], x3.at[p % m3], x3ss.at[p % m3], x3r.at[p % m3], p).wait_recv()
        return 0

    lax.fori_loop(1, m3, get_x3, 0)
    y3 = mm(s3 - jnp.sum(x3[...], axis=0), inv3, NT)
    t2 = mm(y3, c2t, NN)
    x2s[...] = t2
    copy2 = remote(x2s, x2, ps.at[1], pr.at[1], partner(m3))
    copy2.start()

    wide(g1, g1s, g1r, g1f, "pass")

    copy2.wait_recv()
    y2 = mm(s2 - t2 - x2[...], inv2, NT)
    t1 = mm(y2, c1t, NN)
    x1s[...] = t1
    copy1 = remote(x1s, x1, ps.at[2], pr.at[2], partner(m2))
    copy1.start()

    wide(g1, g1s, g1r, g1f, "recv")
    inv0_copy.wait_recv()
    c0t = g1[:, :, :n0].reshape(m1 * sr, n0)
    pair0 = jnp.concatenate([inv0[...], inv0_other[...]], 0)
    hmat = mm(pair0, c0t, NT)
    hg[me % m1] = hmat
    wide(hg, hss, hsr, hf, "start")
    inv1 = g1[:, :, n0:n0 + n1].reshape(m1 * sr, n1)
    s01 = g1[:, :, n0 + n1:].reshape(m1 * sr, 2 * nrhs)
    s1 = jnp.transpose(s01[:, nrhs:])
    second = me // m1 == 1
    mine0 = jnp.where(second, pair0[:, n1:], pair0[:, :n1])
    base = mm(mine0, s01[:, :nrhs], NN)

    copy1.wait_recv()
    y1 = mm(s1 - t1 - x1[...], inv1, NT)
    part = base - mm(hmat, y1, NT)
    eight = sr // 2
    x0s[...] = jnp.concatenate([part[sr:sr + eight], part[sr + eight:]], 1)
    copy0 = remote(x0s, x0, ps.at[3], pr.at[3], other0)
    copy0.start()
    copy0.wait_recv()
    y0[me] = jnp.concatenate([part[:eight], part[eight:sr]], 1) + x0[...]

    def y_copy(j, arriving):
        p = (me + j) % devices
        slot = p if arriving else me
        return remote(y0.at[me], y0.at[slot], ys.at[p], yr.at[slot], p)

    def send_y(j, _):
        y_copy(j, False).start()
        return 0

    lax.fori_loop(1, devices, send_y, 0)
    wide(hg, hss, hsr, hf, "pass")
    lax.fori_loop(1, devices, send_block, 0)

    def get_block(j, _):
        block_copy(j, True).wait_recv()
        return 0

    def get_y(j, _):
        y_copy(j, True).wait_recv()
        return 0

    lax.fori_loop(1, devices, get_y, 0)
    wide(hg, hss, hsr, hf, "recv")

    z1 = y1
    for far in range(2):
        where_ = (me // m1 + far) % 2 * m1
        turned = jnp.transpose(y0[pl.ds(where_, m1)].reshape(m1 * eight, 2 * nrhs))
        for side in range(2):
            piece = hg[:, far * sr + side * eight:far * sr + (side + 1) * eight, :].reshape(m1 * eight, n1)
            z1 = z1 - mm(turned[side * nrhs:(side + 1) * nrhs], piece, NN)

    sol1 = mm(z1, inv1, NN)
    sol2 = mm(y2 - mm(sol1, c1t, NT), inv2, NN)
    sol3 = mm(y3 - mm(sol2, c2t, NT), inv3, NN)
    leaf_out[...] = mm_split(leaf_y - mm(sol3, coup, NN), lhigh[...], llow[...], NN)

    lax.fori_loop(1, devices, get_block, 0)
    full = jnp.transpose(y0[...].reshape(devices * eight, 2 * nrhs))
    sol0 = None
    for side in range(2):
        piece = blocks[:, side * eight:(side + 1) * eight, :].reshape(devices * eight, sr)
        term = mm(full[side * nrhs:(side + 1) * nrhs], piece, NN)
        sol0 = term if sol0 is None else sol0 + term
    sep_out[0] = jnp.transpose(sol0)
    for level, value, size in ((1, sol1, m1), (2, sol2, m2), (3, sol3, m3)):
        width = value.shape[1]
        chosen = jnp.where(iota((sr, width), 1) == me % size * sr + iota((sr, width), 0), 1.0, 0.0).astype(BF16)
        a = value.astype(BF16)
        left = value - a.astype(F32)
        b = left.astype(BF16)
        c = (left - b.astype(F32)).astype(BF16)
        sep_out[level] = raw(chosen, a, NT) + raw(chosen, b, NT) + raw(chosen, c, NT)

    def sent(j, _):
        p = (me + j) % devices
        for copy in load_copies(p, me, me):
            copy.wait_send()
        block_copy(j, False).wait_send()
        y_copy(j, False).wait_send()
        return 0

    lax.fori_loop(1, devices, sent, 0)
    group(g3.at[me % m3], g3, g3s, g3r, m3, "sent")
    group(g2.at[me % m2], g2, g2s, g2r, m2, "sent")
    wide(g1, g1s, g1r, g1f, "sent")
    wide(hg, hss, hsr, hf, "sent")

    def sent_x3(j, _):
        p = me // m3 * m3 + (me + j) % m3
        remote(x3.at[me % m3], x3.at[me % m3], x3ss.at[p % m3], x3r.at[me % m3], p).wait_send()
        return 0

    lax.fori_loop(1, m3, sent_x3, 0)
    for copy in (inv0_copy, copy2, copy1, copy0):
        copy.wait_send()


def shards(
    elem_loads, elem_owner, elem_row, sep_loads, leaf_inverse, leaf_coupling,
    coupling0, coupling1, coupling2, inverse0, inverse1, inverse2, inverse3,
):
    front = lax.axis_size("front")
    devices = lax.axis_size(AXES)
    nrhs, elems = elem_loads.shape
    leaf = leaf_inverse.shape[0]
    sr = sep_loads.shape[2]
    sizes = (inverse0.shape[1], inverse1.shape[1], inverse2.shape[1], inverse3.shape[1])
    n0, n1, n2, n3 = sizes
    cap = 2 * elems // devices
    half = max(8, -(-cap // 16) * 8)
    m1, m2, m3 = devices // 2, devices // 4, devices // 8
    pad = 2 * nrhs
    vmem = pl.BlockSpec(memory_space=pltpu.VMEM)
    dma = pltpu.SemaphoreType.DMA
    V = pltpu.VMEM
    leaf_solution, sep_solution = pl.pallas_call(
        functools.partial(kernel, devices, front, sr, sizes, cap, half),
        out_shape=(
            jax.ShapeDtypeStruct((nrhs, leaf), F32),
            jax.ShapeDtypeStruct((sep_loads.shape[0], sr, nrhs), F32),
        ),
        in_specs=[vmem] * 11 + [pl.BlockSpec(memory_space=pl.ANY), vmem],
        out_specs=(vmem, vmem),
        scratch_shapes=[
            V((leaf, leaf), F32), V((leaf, leaf), BF16), V((leaf, leaf), BF16),
            V((devices, half, 2 * nrhs), F32), V((devices, 1, 128), F32),
            V((devices, half, 2 * nrhs), F32), V((devices, 1, 128), F32),
            V((m1, sr, n0 + n1 + pad), F32), V((m2, sr, n1 + n2 + pad), F32), V((m3, sr, n2 + n3 + nrhs), F32),
            V((devices, sr, sr), F32),
            V((devices, sr, sr), F32), V((sr, n0), F32),
            V((m3, nrhs, n3), F32), V((nrhs, n2), F32), V((nrhs, n1), F32), V((sr // 2, 2 * nrhs), F32),
            V((nrhs, n2), F32), V((nrhs, n1), F32), V((sr // 2, 2 * nrhs), F32),
            V((m1, 2 * sr, n1), F32), V((devices, sr // 2, 2 * nrhs), F32),
            dma((1,)), dma((devices,)), dma((devices,)), dma((devices,)), dma((devices,)),
            dma((m1,)), dma((m1,)), dma((m2,)), dma((m2,)), dma((m3,)), dma((m3,)),
            dma((devices,)), dma((devices,)), dma((m1,)), dma((m1,)), dma((devices,)), dma((devices,)),
            dma((m3,)), dma((m3,)), dma((4,)), dma((4,)), dma((m1,)), dma((m1,)),
        ],
        compiler_params=pltpu.CompilerParams(
            collective_id=0, has_side_effects=True, vmem_limit_bytes=60 * 1024 * 1024),
    )(elem_loads, elem_owner.T, elem_row.reshape(1, elems), jnp.swapaxes(sep_loads, 1, 2),
      inverse0, inverse1, inverse2, inverse3, coupling0.T, coupling1.T, coupling2.T,
      leaf_inverse, leaf_coupling)
    return leaf_solution, jnp.swapaxes(sep_solution, 1, 2)


def solution(mesh):
    in_specs = (
        P(None, AXES), P(AXES, None), P(AXES), P(None, None, AXES), P(AXES, None), P(None, AXES),
        P(None, AXES), P(None, AXES), P(None, AXES),
        P(AXES, None), P(AXES, None), P(AXES, None), P(AXES, None),
    )
    out_specs = (P(None, AXES), P(None, None, AXES))
    return jax.shard_map(shards, mesh=mesh, in_specs=in_specs, out_specs=out_specs, check_vma=False)
```

```python
import functools
import jax
import jax.numpy as jnp
from jax import lax
from jax.experimental import pallas as pl
from jax.experimental.pallas import tpu as pltpu
from jax.sharding import PartitionSpec as P

F32 = jnp.float32
BF16 = jnp.bfloat16
AXES = ("cube", "front")
MESH = pl.DeviceIdType.MESH

NN = ((1,), (0,))
NT = ((1,), (1,))
TN = ((0,), (0,))


def raw(a, b, dims):
    return lax.dot_general(a, b, (dims, ((), ())), preferred_element_type=F32)


def split(x):
    high = x.astype(BF16)
    return high, (x - high.astype(F32)).astype(BF16)


def mm_split(a, high, low, dims):
    a_high, a_low = split(a)
    rows = a.shape[0]
    both = raw(jnp.concatenate([a_high, a_low], 0), high, dims)
    return both[:rows] + both[rows:] + raw(a_high, low, dims)


def mm(a, b, dims):
    high, low = split(b)
    return mm_split(a, high, low, dims)


def iota(shape, dim):
    return lax.broadcasted_iota(jnp.int32, shape, dim)


def kernel(
    devices, front, sr, sizes, cap, half,
    vals, owner, rows, sep, inv0, inv1_own, inv2_own, inv3_own, coup0, coup1, coup2, leaf_inv, leaf_coup,
    leaf_out, sep_out,
    linv, lhigh, llow, sendv, sendi, recvv, recvi, g1, g2, g3, inv0_blocks, blocks, inv0_other,
    x3, x2, x1, x0, x2s, x1s, x0s, hg, y0,
    lsem, vs, vr, is_, ir, g1s, g1r, g2s, g2r, g3s, g3r, bs, br, hss, hsr, ys, yr, x3ss, x3r, ps, pr, g1f, hf,
):
    n0, n1, n2, n3 = sizes
    me = lax.axis_index("cube") * front + lax.axis_index("front")
    m1, m2, m3 = devices // 2, devices // 4, devices // 8
    nrhs = vals.shape[0]
    leaf = leaf_coup.shape[1]
    elems = vals.shape[1]

    def dev(p):
        return (p // front, p % front)

    def partner(bit):
        return me + bit * (1 - 2 * ((me // bit) % 2))

    def remote(src, dst, ssem, rsem, p):
        return pltpu.make_async_remote_copy(
            src_ref=src, dst_ref=dst, send_sem=ssem, recv_sem=rsem,
            device_id=dev(p), device_id_type=MESH)

    fetch = pltpu.make_async_copy(leaf_inv, linv, lsem.at[0])
    fetch.start()

    barrier = pltpu.get_barrier_semaphore()

    def greet(j, _):
        pl.semaphore_signal(barrier, inc=1, device_id=dev((me + j) % devices), device_id_type=MESH)
        return 0

    lax.fori_loop(1, devices, greet, 0)

    own = owner[...]
    marks = iota((devices, elems), 0) == own
    marks_f = jnp.where(marks, 1.0, 0.0).astype(F32)
    earlier = jnp.where(iota((elems, elems), 0) < iota((elems, elems), 1), 1.0, 0.0).astype(BF16)
    before = raw(marks_f.astype(BF16), earlier, NN)
    rank = jnp.sum(before * marks_f, axis=0, keepdims=True).astype(jnp.int32)
    v = vals[...]
    v_a = v.astype(BF16)
    rest = v - v_a.astype(F32)
    v_b = rest.astype(BF16)
    v_c = (rest - v_b.astype(F32)).astype(BF16)
    place = iota((devices * half, elems), 0)
    sides = []
    for side in range(2):
        low = side * half
        target = jnp.where((rank >= low) & (rank < low + half), own * half + rank - low, -1)
        hot = jnp.where(place == target, 1.0, 0.0).astype(BF16)
        sides.append(raw(hot, v_a, NT) + raw(hot, v_b, NT) + raw(hot, v_c, NT))
    sendv[...] = jnp.concatenate(sides, 1).reshape(sendv.shape)
    number = rows[...].astype(F32)
    upper = jnp.floor(number * 0.0078125)
    lower = number - upper * 128.0
    ranks = jnp.where(iota((128, elems), 0) == rank, 1.0, 0.0).astype(BF16)
    sendi[...] = (
        raw((marks_f * upper).astype(BF16), ranks, NT) * 128.0
        + raw((marks_f * lower).astype(BF16), ranks, NT)
    ).reshape(sendi.shape)
    g1[me % m1] = jnp.concatenate(
        [coup0[...], inv1_own[...], sep[0], sep[1]], 1)
    g2[me % m2] = jnp.concatenate([coup1[...], inv2_own[...], sep[2], sep[2]], 1)
    g3[me % m3] = jnp.concatenate([coup2[...], inv3_own[...], sep[3]], 1)
    recvv[me] = sendv[me]
    recvi[me] = sendi[me]

    pl.semaphore_wait(barrier, devices - 1)

    def load_copies(p, slot, sem):
        return (
            remote(sendv.at[p], recvv.at[slot], vs.at[p], vr.at[sem], p),
            remote(sendi.at[p], recvi.at[slot], is_.at[p], ir.at[sem], p),
        )

    def send_loads(j, _):
        for copy in load_copies((me + j) % devices, me, me):
            copy.start()
        return 0

    lax.fori_loop(1, devices, send_loads, 0)

    def group_copy(src, dst, ssem, rsem, size, j, arriving):
        p = me // size * size + (me + j) % size
        slot = p % size if arriving else me % size
        return remote(src, dst.at[slot], ssem.at[p % size], rsem.at[slot], p)

    def group(src, dst, ssem, rsem, size, act):
        def body(j, _):
            copy = group_copy(src, dst, ssem, rsem, size, j, act != "start")
            if act == "start":
                copy.start()
            elif act == "recv":
                copy.wait_recv()
            else:
                copy.wait_send()
            return 0
        lax.fori_loop(1, size, body, 0)

    other0 = partner(m1)
    inv0_copy = remote(inv0, inv0_other, ps.at[0], pr.at[0], other0)

    group(g3.at[me % m3], g3, g3s, g3r, m3, "start")
    group(g2.at[me % m2], g2, g2s, g2r, m2, "start")
    inv0_copy.start()
    twin = partner(1)

    def wide(dst, ssem, rsem, fsem, act):
        start = me // m1 * m1

        def slot_of(first, j):
            return (first % m1 + front * j) % m1

        def direct(j, _):
            slot = slot_of(me, j)
            if act == "start":
                remote(dst.at[me % m1], dst.at[me % m1], ssem.at[slot], rsem.at[me % m1], start + slot).start()
            elif act == "sent":
                remote(dst.at[me % m1], dst.at[me % m1], ssem.at[slot], rsem.at[me % m1], start + slot).wait_send()
            elif act == "pass":
                remote(dst.at[slot], dst.at[slot], ssem.at[slot], rsem.at[slot], start + slot).wait_recv()
                remote(dst.at[slot], dst.at[slot], fsem.at[slot], rsem.at[slot], twin).start()
            return 0

        def passed(j, _):
            if act == "sent":
                slot = slot_of(me, j)
                remote(dst.at[slot], dst.at[slot], fsem.at[slot], rsem.at[slot], twin).wait_send()
            else:
                slot = slot_of(twin, j)
                remote(dst.at[slot], dst.at[slot], fsem.at[slot], rsem.at[slot], twin).wait_recv()
            return 0

        if act == "start":
            mine = me % m1
            remote(dst.at[mine], dst.at[mine], fsem.at[mine], rsem.at[mine], twin).start()
        if act != "recv":
            lax.fori_loop(1, m1 // front, direct, 0)
        if act in ("recv", "sent"):
            lax.fori_loop(0, m1 // front, passed, 0)

    wide(g1, g1s, g1r, g1f, "start")

    def block_copy(j, arriving):
        p = (me + j) % devices
        slot = p if arriving else me
        return remote(inv0_blocks.at[p], blocks.at[slot], bs.at[p], br.at[slot], p)

    def send_block(j, _):
        block_copy(j, False).start()
        return 0

    inv0_value = inv0[...]
    for p in range(devices):
        inv0_blocks[p] = inv0_value[:, p * sr:(p + 1) * sr]
    blocks[me] = inv0_blocks[me]

    fetch.wait()
    linv_value = linv[...]
    high = linv_value.astype(BF16)
    lhigh[...] = high
    llow[...] = (linv_value - high.astype(F32)).astype(BF16)

    def get_loads(j, _):
        p = (me + j) % devices
        for copy in load_copies(p, p, p):
            copy.wait_recv()
        return 0

    lax.fori_loop(1, devices, get_loads, 0)

    slots = devices * half
    arrived = jnp.transpose(recvv[...].reshape(slots, 128))
    pick = jnp.where(iota((slots, devices), 0) // half == iota((slots, devices), 1), 1.0, 0.0).astype(BF16)
    ids = recvi[...].reshape(devices, 128)
    ids_up = jnp.floor(ids * 0.0078125)
    ids_low = ids - ids_up * 128.0
    spread = raw(pick, ids_up.astype(BF16), NN) * 128.0 + raw(pick, ids_low.astype(BF16), NN)
    lane = iota((slots, 128), 1)
    turn = iota((slots, 128), 0) % half
    loads = None
    for side in range(2):
        row = jnp.sum(jnp.where(lane == turn + side * half, spread, 0.0), axis=1, keepdims=True)
        hot = jnp.where(iota((slots, leaf), 1) == row.astype(jnp.int32), 1.0, 0.0).astype(BF16)
        part_high, part_low = split(arrived[side * nrhs:(side + 1) * nrhs])
        both = raw(jnp.concatenate([part_high, part_low], 0), hot, NN)
        term = both[:nrhs] + both[nrhs:]
        loads = term if loads is None else loads + term
    leaf_y = mm_split(loads, lhigh[...], llow[...], NT)
    coup = leaf_coup[...]
    x3[me % m3] = mm(leaf_y, coup, NT)
    group(x3.at[me % m3], x3, x3ss, x3r, m3, "start")

    group(g3.at[me % m3], g3, g3s, g3r, m3, "recv")
    c2t = g3[:, :, :n2].reshape(m3 * sr, n2)
    inv3 = g3[:, :, n2:n2 + n3].reshape(m3 * sr, n3)
    inv3_s = split(inv3)
    s3 = jnp.transpose(g3[:, :, n2 + n3:].reshape(m3 * sr, nrhs))
    j3 = mm(jnp.transpose(inv3), c2t, NN)
    j3_s = split(j3)
    group(g2.at[me % m2], g2, g2s, g2r, m2, "recv")
    c1t = g2[:, :, :n1].reshape(m2 * sr, n1)
    inv2 = g2[:, :, n1:n1 + n2].reshape(m2 * sr, n2)
    s2 = jnp.transpose(g2[:, :, n1 + n2:n1 + n2 + nrhs].reshape(m2 * sr, nrhs))

    def get_x3(j, _):
        p = me // m3 * m3 + (me + j) % m3
        remote(x3.at[me % m3], x3.at[p % m3], x3ss.at[p % m3], x3r.at[p % m3], p).wait_recv()
        return 0

    lax.fori_loop(1, m3, get_x3, 0)
    r3 = s3 - jnp.sum(x3[...], axis=0)
    t2 = mm_split(r3, *j3_s, NN)
    x2s[...] = t2
    copy2 = remote(x2s, x2, ps.at[1], pr.at[1], partner(m3))
    copy2.start()

    j2 = mm(jnp.transpose(inv2), c1t, NN)
    j2_s = split(j2)
    r2_base = s2 - t2
    y3 = mm_split(r3, *inv3_s, NT)
    q3 = mm_split(y3, *inv3_s, NN)
    wide(g1, g1s, g1r, g1f, "pass")

    copy2.wait_recv()
    r2 = r2_base - x2[...]
    t1 = mm_split(r2, *j2_s, NN)
    x1s[...] = t1
    copy1 = remote(x1s, x1, ps.at[2], pr.at[2], partner(m2))
    copy1.start()

    wide(g1, g1s, g1r, g1f, "recv")
    inv0_copy.wait_recv()
    c0t = g1[:, :, :n0].reshape(m1 * sr, n0)
    pair0 = jnp.concatenate([inv0[...], inv0_other[...]], 0)
    inv1_s = split(g1[:, :, n0:n0 + n1].reshape(m1 * sr, n1))
    k1 = mm_split(mm(pair0, c0t, NT), *inv1_s, NN)
    hg[me % m1] = k1
    wide(hg, hss, hsr, hf, "start")
    s01 = g1[:, :, n0 + n1:].reshape(m1 * sr, 2 * nrhs)
    s1 = jnp.transpose(s01[:, nrhs:]) - t1
    second = me // m1 == 1
    mine0 = jnp.where(second, pair0[:, n1:], pair0[:, :n1])
    base = mm(mine0, s01[:, :nrhs], NN)

    copy1.wait_recv()
    r1 = s1 - x1[...]
    part = base - mm(k1, r1, NT)
    eight = sr // 2
    x0s[...] = jnp.concatenate([part[sr:sr + eight], part[sr + eight:]], 1)
    copy0 = remote(x0s, x0, ps.at[3], pr.at[3], other0)
    copy0.start()
    inv2_s = split(inv2)
    q2 = mm_split(mm_split(r2, *inv2_s, NT), *inv2_s, NN)
    q1 = mm_split(mm_split(r1, *inv1_s, NT), *inv1_s, NN)
    copy0.wait_recv()
    y0[me] = jnp.concatenate([part[:eight], part[eight:sr]], 1) + x0[...]

    def y_copy(j, arriving):
        p = (me + j) % devices
        slot = p if arriving else me
        return remote(y0.at[me], y0.at[slot], ys.at[p], yr.at[slot], p)

    def send_y(j, _):
        y_copy(j, False).start()
        return 0

    lax.fori_loop(1, devices, send_y, 0)
    wide(hg, hss, hsr, hf, "pass")
    lax.fori_loop(1, devices, send_block, 0)
    swept = mm_split(jnp.concatenate([leaf_y, coup], 0), lhigh[...], llow[...], NN)
    leaf_base = swept[:nrhs]
    lift_s = split(swept[nrhs:])
    j23_s = split(mm(j3, j2, NN))
    q32 = q3 - mm_split(q2, *j3_s, NT)
    wide(hg, hss, hsr, hf, "recv")
    pieces = []
    for far in range(2):
        for side in range(2):
            low = far * sr + side * eight
            pieces.append(hg[:, low:low + eight, :].reshape(m1 * eight, n1))
    k1_s = split(jnp.concatenate(pieces, 0))

    def get_block(j, _):
        block_copy(j, True).wait_recv()
        return 0

    def get_y(j, _):
        y_copy(j, True).wait_recv()
        return 0

    lax.fori_loop(1, devices, get_y, 0)

    parts = []
    for far in range(2):
        where_ = (me // m1 + far) % 2 * m1
        turned = jnp.transpose(y0[pl.ds(where_, m1)].reshape(m1 * eight, 2 * nrhs))
        parts += [turned[:nrhs], turned[nrhs:]]
    sol1 = q1 - mm_split(jnp.concatenate(parts, 1), *k1_s, NN)
    sol3 = q32 + mm_split(sol1, *j23_s, NT)
    leaf_out[...] = leaf_base - mm_split(sol3, *lift_s, NN)
    sol2 = q2 - mm_split(sol1, *j2_s, NT)

    lax.fori_loop(1, devices, get_block, 0)
    full = jnp.transpose(y0[...].reshape(devices * eight, 2 * nrhs))
    sol0 = None
    for side in range(2):
        piece = blocks[:, side * eight:(side + 1) * eight, :].reshape(devices * eight, sr)
        term = mm(full[side * nrhs:(side + 1) * nrhs], piece, NN)
        sol0 = term if sol0 is None else sol0 + term
    sep_out[0] = jnp.transpose(sol0)
    for level, value, size in ((1, sol1, m1), (2, sol2, m2), (3, sol3, m3)):
        width = value.shape[1]
        chosen = jnp.where(iota((sr, width), 1) == me % size * sr + iota((sr, width), 0), 1.0, 0.0).astype(BF16)
        a = value.astype(BF16)
        left = value - a.astype(F32)
        b = left.astype(BF16)
        c = (left - b.astype(F32)).astype(BF16)
        sep_out[level] = raw(chosen, a, NT) + raw(chosen, b, NT) + raw(chosen, c, NT)

    def sent(j, _):
        p = (me + j) % devices
        for copy in load_copies(p, me, me):
            copy.wait_send()
        block_copy(j, False).wait_send()
        y_copy(j, False).wait_send()
        return 0

    lax.fori_loop(1, devices, sent, 0)
    group(g3.at[me % m3], g3, g3s, g3r, m3, "sent")
    group(g2.at[me % m2], g2, g2s, g2r, m2, "sent")
    wide(g1, g1s, g1r, g1f, "sent")
    wide(hg, hss, hsr, hf, "sent")

    def sent_x3(j, _):
        p = me // m3 * m3 + (me + j) % m3
        remote(x3.at[me % m3], x3.at[me % m3], x3ss.at[p % m3], x3r.at[me % m3], p).wait_send()
        return 0

    lax.fori_loop(1, m3, sent_x3, 0)
    for copy in (inv0_copy, copy2, copy1, copy0):
        copy.wait_send()


def shards(
    elem_loads, elem_owner, elem_row, sep_loads, leaf_inverse, leaf_coupling,
    coupling0, coupling1, coupling2, inverse0, inverse1, inverse2, inverse3,
):
    front = lax.axis_size("front")
    devices = lax.axis_size(AXES)
    nrhs, elems = elem_loads.shape
    leaf = leaf_inverse.shape[0]
    sr = sep_loads.shape[2]
    sizes = (inverse0.shape[1], inverse1.shape[1], inverse2.shape[1], inverse3.shape[1])
    n0, n1, n2, n3 = sizes
    cap = 2 * elems // devices
    half = max(8, -(-cap // 16) * 8)
    m1, m2, m3 = devices // 2, devices // 4, devices // 8
    pad = 2 * nrhs
    vmem = pl.BlockSpec(memory_space=pltpu.VMEM)
    dma = pltpu.SemaphoreType.DMA
    V = pltpu.VMEM
    leaf_solution, sep_solution = pl.pallas_call(
        functools.partial(kernel, devices, front, sr, sizes, cap, half),
        out_shape=(
            jax.ShapeDtypeStruct((nrhs, leaf), F32),
            jax.ShapeDtypeStruct((sep_loads.shape[0], sr, nrhs), F32),
        ),
        in_specs=[vmem] * 11 + [pl.BlockSpec(memory_space=pl.ANY), vmem],
        out_specs=(vmem, vmem),
        scratch_shapes=[
            V((leaf, leaf), F32), V((leaf, leaf), BF16), V((leaf, leaf), BF16),
            V((devices, half, 2 * nrhs), F32), V((devices, 1, 128), F32),
            V((devices, half, 2 * nrhs), F32), V((devices, 1, 128), F32),
            V((m1, sr, n0 + n1 + pad), F32), V((m2, sr, n1 + n2 + pad), F32), V((m3, sr, n2 + n3 + nrhs), F32),
            V((devices, sr, sr), F32),
            V((devices, sr, sr), F32), V((sr, n0), F32),
            V((m3, nrhs, n3), F32), V((nrhs, n2), F32), V((nrhs, n1), F32), V((sr // 2, 2 * nrhs), F32),
            V((nrhs, n2), F32), V((nrhs, n1), F32), V((sr // 2, 2 * nrhs), F32),
            V((m1, 2 * sr, n1), F32), V((devices, sr // 2, 2 * nrhs), F32),
            dma((1,)), dma((devices,)), dma((devices,)), dma((devices,)), dma((devices,)),
            dma((m1,)), dma((m1,)), dma((m2,)), dma((m2,)), dma((m3,)), dma((m3,)),
            dma((devices,)), dma((devices,)), dma((m1,)), dma((m1,)), dma((devices,)), dma((devices,)),
            dma((m3,)), dma((m3,)), dma((4,)), dma((4,)), dma((m1,)), dma((m1,)),
        ],
        compiler_params=pltpu.CompilerParams(
            collective_id=0, has_side_effects=True, vmem_limit_bytes=60 * 1024 * 1024),
    )(elem_loads, elem_owner.T, elem_row.reshape(1, elems), jnp.swapaxes(sep_loads, 1, 2),
      inverse0, inverse1, inverse2, inverse3, coupling0.T, coupling1.T, coupling2.T,
      leaf_inverse, leaf_coupling)
    return leaf_solution, jnp.swapaxes(sep_solution, 1, 2)


def solution(mesh):
    in_specs = (
        P(None, AXES), P(AXES, None), P(AXES), P(None, None, AXES), P(AXES, None), P(None, AXES),
        P(None, AXES), P(None, AXES), P(None, AXES),
        P(AXES, None), P(AXES, None), P(AXES, None), P(AXES, None),
    )
    out_specs = (P(None, AXES), P(None, None, AXES))
    return jax.shard_map(shards, mesh=mesh, in_specs=in_specs, out_specs=out_specs, check_vma=False)
```
